32 devices in a mesh: dp: 16 (over z, y, x), tensor: 2 (over core).
Axes of the slice: x: 2, y: 2, z: 4, core: 2. Of those that a mesh axis runs over, the one named last changes fastest.
Arguments:
- tokens: bfloat16 [8192, 1024], P(('dp', 'tensor')), may hold values from -6 to 6
- segment_ids: int32 [8192], P('dp'), may hold values from 0 to 2, as said below
- positions: int32 [8192], P('dp'), may hold values from 0 to 2047, as said below
- norm1_gain: float32 [1024], replicated, may hold values from 0.25 to 1.75
- qkv_weight: bfloat16 [1024, 3, 1024], P(None, None, 'tensor'), may hold values from -0.1875 to 0.1875
- out_weight: bfloat16 [1024, 1024], P('tensor'), may hold values from -1.5 to 1.5
- norm2_gain: float32 [1024], replicated, may hold values from 0.25 to 1.75
- mlp_in_weight: bfloat16 [1024, 2, 2624], P(None, None, 'tensor'), may hold values from -0.1875 to 0.1875
- mlp_out_weight: bfloat16 [2624, 1024], P('tensor'), may hold values from -0.125 to 0.125
- cotangent: bfloat16 [8192, 1024], P(('dp', 'tensor')), may hold values from -6 to 6
Outputs:
- output: bfloat16 [8192, 1024], P(('dp', 'tensor'))
- input_grad: bfloat16 [8192, 1024], P(('dp', 'tensor'))
- norm1_gain_grad: float32 [1024], replicated
- qkv_weight_grad: float32 [1024, 3, 1024], P(None, None, 'tensor')
- out_weight_grad: float32 [1024, 1024], P('tensor')
- norm2_gain_grad: float32 [1024], replicated
- mlp_in_weight_grad: float32 [1024, 2, 2624], P(None, None, 'tensor')
- mlp_out_weight_grad: float32 [2624, 1024], P('tensor')
The draws below stay inside these ranges and needn't reach their ends.
Inputs may be any that keep to these rules, and one draw needn't show every extreme that they name: Within each sequence of 512 tokens segment_ids never falls and rises by at most one per step; tokens attend only to tokens of the same sequence and segment. Inside a segment positions rise by one per token; a segment that begins a sequence starts at a position of at most 1536, every later one starts at 0.
All inputs are finite; a program needn't handle non-finite values.
Results may differ from the reference program's by a relative error of at most 0.02.
Values may be sent and summed in bfloat16 or wider, within the bound.
A program may use at most 128 MiB of HBM per device.

```python
import math
import jax
import jax.numpy as jnp
from jax import lax

D = 1024
HEADS = 16
HEAD_DIM = 64
FF = 2624
SEQ_LEN = 512
SEQS = 16
TOKENS = 8192


def boundary_cuts(key):
    base_key = jax.random.fold_in(key, 11)
    key_one, key_two, key_three = jax.random.split(base_key, 3)
    cut_one = jax.random.randint(key_one, (SEQS,), 0, SEQ_LEN)
    cut_two = cut_one + jax.random.randint(key_two, (SEQS,), 2 * SEQ_LEN // 5, 4 * SEQ_LEN)
    offset = jax.random.randint(key_three, (SEQS,), 0, 3 * SEQ_LEN)
    index = jnp.arange(SEQS, dtype=jnp.int32)
    first = index == 0
    last = index == SEQS - 1
    cut_one = jnp.where(first, SEQ_LEN // 4, jnp.where(last, SEQ_LEN, cut_one))
    cut_two = jnp.where(first, SEQ_LEN // 2, jnp.where(last, 2 * SEQ_LEN, cut_two))
    offset = jnp.where(last, 3 * SEQ_LEN, offset)
    return (cut_one, cut_two, offset)


def draw_segment_ids(key, part):
    cut_one, cut_two, offset = boundary_cuts(key)
    places = jnp.arange(SEQ_LEN, dtype=jnp.int32)[None, :]
    labels = (places >= cut_one[:, None]).astype(jnp.int32) + (places >= cut_two[:, None]).astype(jnp.int32)
    return labels.reshape(TOKENS)


def draw_positions(key, part):
    cut_one, cut_two, offset = boundary_cuts(key)
    places = jnp.arange(SEQ_LEN, dtype=jnp.int32)[None, :]
    counted = jnp.where(places < cut_one[:, None], offset[:, None] + places, jnp.where(places < cut_two[:, None], places - cut_one[:, None], places - cut_two[:, None]))
    return counted.astype(jnp.int32).reshape(TOKENS)


def steps_of(own_key, extent, cuts, least, top_value):
    def one(position, shards_of):
        steps = jax.random.uniform(jax.random.fold_in(jax.random.fold_in(own_key, 6), position), (shards_of,), jnp.float32, least / len(cuts), top_value / len(cuts))
        return jnp.repeat(jnp.exp(steps), extent[position] // shards_of).reshape((-1,) + (1,) * (len(extent) - position - 1))

    level = one(*cuts[0])
    for cut in cuts[1:]:
        level = level * one(*cut)
    return level


def centred(rng, extent, spread, most, pieces=(), held_as=jnp.bfloat16):
    array = spread * jax.random.normal(rng, extent, jnp.float32)
    if pieces:
        array = array * steps_of(rng, extent, pieces, -0.22, 0.18)
    return jnp.clip(array, -most, most).astype(held_as)


def setup_inputs(seed: int = 0) -> dict:
    key_list = jax.random.split(jax.random.key(seed), 11)
    return {
        "tokens": centred(key_list[0], (TOKENS, D), 1.0, 6.0, ((0, 32),)),
        "segment_ids": draw_segment_ids(jax.random.fold_in(key_list[10], 71), 0),
        "positions": draw_positions(jax.random.fold_in(key_list[10], 71), 0),
        "norm1_gain": jnp.clip(1.0 + 0.15 * jax.random.normal(key_list[3], (D,), jnp.float32), 0.25, 1.75),
        "qkv_weight": centred(key_list[4], (D, 3, HEADS * HEAD_DIM), D ** -0.5, 0.1875, ((2, 2),)),
        "out_weight": centred(key_list[5], (HEADS * HEAD_DIM, D), (HEADS * HEAD_DIM // 64) ** -0.5, 1.5, ((0, 2),)),
        "norm2_gain": jnp.clip(1.0 + 0.15 * jax.random.normal(key_list[6], (D,), jnp.float32), 0.25, 1.75),
        "mlp_in_weight": centred(key_list[7], (D, 2, FF), D ** -0.5, 0.1875, ((2, 2),)),
        "mlp_out_weight": centred(key_list[8], (FF, D), FF ** -0.5, 0.125, ((0, 2),)),
        "cotangent": centred(key_list[9], (TOKENS, D), 1.0, 6.0, ((0, 32),)),
    }


EPS = 1e-05
THETA = 160000.0
NEG_FILL = -1e+30
INV_ROOT_TWO_PI = 0.3989422804014327

def norm_rows(rows):
    centered = rows - lax.optimization_barrier(jnp.mean(rows, axis=-1, keepdims=True))
    inv_spread = lax.rsqrt(lax.optimization_barrier(jnp.mean(centered * centered, axis=-1, keepdims=True)) + EPS)
    return (centered * inv_spread, inv_spread)

def norm_back(grad_rows, normed, inv_spread):
    return inv_spread * (grad_rows - lax.optimization_barrier(jnp.mean(grad_rows, axis=-1, keepdims=True)) - normed * lax.optimization_barrier(jnp.mean(grad_rows * normed, axis=-1, keepdims=True)))

def rope_tables(position_ids):
    half_dim = HEAD_DIM // 2
    freqs = jnp.exp(-math.log(THETA) * (jnp.arange(half_dim, dtype=jnp.float32) * 2.0 / HEAD_DIM))
    angles = position_ids.astype(jnp.float32)[:, None] * freqs[None, :]
    cos_table = jnp.concatenate([jnp.cos(angles), jnp.cos(angles)], axis=-1)[:, None, :]
    sin_table = jnp.concatenate([jnp.sin(angles), jnp.sin(angles)], axis=-1)[:, None, :]
    return (cos_table, sin_table)

def rotate(values, cos_table, sin_table):
    half_dim = HEAD_DIM // 2
    turned = jnp.concatenate([-values[..., half_dim:], values[..., :half_dim]], axis=-1)
    return values * cos_table + turned * sin_table

def unrotate(grads, cos_table, sin_table):
    half_dim = HEAD_DIM // 2
    weighted = grads * sin_table
    turned = jnp.concatenate([weighted[..., half_dim:], -weighted[..., :half_dim]], axis=-1)
    return grads * cos_table + turned

def attend(query, key_rot, value, seg_row):
    scale = HEAD_DIM ** (-0.5)
    scores = jnp.einsum('qhd,khd->hqk', query.astype(jnp.float32), key_rot.astype(jnp.float32)) * scale
    allowed = (seg_row[:, None] == seg_row[None, :])[None]
    scores = jnp.where(allowed, scores, NEG_FILL)
    row_max = lax.optimization_barrier(jnp.max(scores, axis=-1))
    expd = jnp.exp(scores - row_max[..., None])
    total = lax.optimization_barrier(jnp.sum(expd, axis=-1))
    log_total = row_max + jnp.log(total)
    probs = (expd / total[..., None]).astype(jnp.bfloat16)
    attended = jnp.einsum('hqk,khd->qhd', probs.astype(jnp.float32), value.astype(jnp.float32))
    return (attended.astype(jnp.bfloat16), log_total)

def attend_back(query, key_rot, value, attended, grad_out, log_total, seg_row):
    scale = HEAD_DIM ** (-0.5)
    scores = jnp.einsum('qhd,khd->hqk', query.astype(jnp.float32), key_rot.astype(jnp.float32)) * scale
    allowed = (seg_row[:, None] == seg_row[None, :])[None]
    probs = jnp.where(allowed, jnp.exp(scores - log_total[..., None]), 0.0)
    probs_low = probs.astype(jnp.bfloat16)
    grad_f32 = grad_out.astype(jnp.float32)
    grad_value = jnp.einsum('hqk,qhd->khd', probs_low.astype(jnp.float32), grad_f32)
    grad_probs = jnp.einsum('qhd,khd->hqk', grad_f32, value.astype(jnp.float32))
    delta = lax.optimization_barrier(jnp.sum(grad_f32 * attended.astype(jnp.float32), axis=-1)).T
    grad_scores = (probs * (grad_probs - delta[..., None]) * scale).astype(jnp.bfloat16)
    grad_query = jnp.einsum('hqk,khd->qhd', grad_scores.astype(jnp.float32), key_rot.astype(jnp.float32))
    grad_key = jnp.einsum('hqk,qhd->khd', grad_scores.astype(jnp.float32), query.astype(jnp.float32))
    return (grad_query, grad_key, grad_value)

def reference(tokens, segment_ids, positions, norm1_gain, qkv_weight, out_weight, norm2_gain, mlp_in_weight, mlp_out_weight, cotangent):
    width_all = HEADS * HEAD_DIM
    qkv_flat = qkv_weight.reshape(D, 3 * width_all)
    mlp_flat = mlp_in_weight.reshape(D, 2 * FF)

    def one_sequence(carry, inputs):
        seq_tokens, seq_segs, seq_pos, seq_cot = inputs
        token_f32 = seq_tokens.astype(jnp.float32)
        normed_one, spread_one = norm_rows(token_f32)
        attn_in = (normed_one * norm1_gain).astype(jnp.bfloat16)
        projected = jnp.dot(attn_in, qkv_flat, preferred_element_type=jnp.float32).reshape(SEQ_LEN, 3, HEADS, HEAD_DIM)
        cos_table, sin_table = rope_tables(seq_pos)
        query = rotate(projected[:, 0], cos_table, sin_table).astype(jnp.bfloat16)
        key_rot = rotate(projected[:, 1], cos_table, sin_table).astype(jnp.bfloat16)
        value = projected[:, 2].astype(jnp.bfloat16)
        attended, log_total = attend(query, key_rot, value, seq_segs)
        attn_flat = attended.reshape(SEQ_LEN, width_all)
        resid_mid = token_f32 + jnp.dot(attn_flat, out_weight, preferred_element_type=jnp.float32)
        normed_two, spread_two = norm_rows(resid_mid)
        mlp_in = (normed_two * norm2_gain).astype(jnp.bfloat16)
        gate_up = jnp.dot(mlp_in, mlp_flat, preferred_element_type=jnp.float32).reshape(SEQ_LEN, 2, FF)
        gate_pre = gate_up[:, 0]
        up_part = gate_up[:, 1]
        activated = jax.nn.gelu(gate_pre, approximate=False)
        hidden = (activated * up_part).astype(jnp.bfloat16)
        result = (resid_mid + jnp.dot(hidden, mlp_out_weight, preferred_element_type=jnp.float32)).astype(jnp.bfloat16)
        cot_f32 = seq_cot.astype(jnp.float32)
        grad_w2 = jnp.dot(hidden.T, seq_cot, preferred_element_type=jnp.float32)
        grad_hidden = jnp.dot(seq_cot, mlp_out_weight.T, preferred_element_type=jnp.float32)
        slope = 0.5 * (1.0 + jax.scipy.special.erf(gate_pre / math.sqrt(2.0))) + gate_pre * jnp.exp(-0.5 * gate_pre * gate_pre) * INV_ROOT_TWO_PI
        grad_gu = jnp.stack([grad_hidden * up_part * slope, grad_hidden * activated], axis=1).astype(jnp.bfloat16).reshape(SEQ_LEN, 2 * FF)
        grad_w1 = jnp.dot(mlp_in.T, grad_gu, preferred_element_type=jnp.float32).reshape(D, 2, FF)
        grad_mlp_in = jnp.dot(grad_gu, mlp_flat.T, preferred_element_type=jnp.float32)
        grad_gain_two = lax.optimization_barrier(jnp.sum(grad_mlp_in * normed_two, axis=0))
        grad_mid = cot_f32 + norm_back(grad_mlp_in * norm2_gain, normed_two, spread_two)
        grad_mid_low = grad_mid.astype(jnp.bfloat16)
        grad_wo = jnp.dot(attn_flat.T, grad_mid_low, preferred_element_type=jnp.float32)
        grad_att = jnp.dot(grad_mid_low, out_weight.T, preferred_element_type=jnp.float32).astype(jnp.bfloat16).reshape(SEQ_LEN, HEADS, HEAD_DIM)
        grad_query, grad_key, grad_value = attend_back(query, key_rot, value, attended, grad_att, log_total, seq_segs)
        grad_proj = jnp.stack([unrotate(grad_query, cos_table, sin_table), unrotate(grad_key, cos_table, sin_table), grad_value], axis=1)
        grad_proj = grad_proj.astype(jnp.bfloat16).reshape(SEQ_LEN, 3 * width_all)
        grad_wqkv = jnp.dot(attn_in.T, grad_proj, preferred_element_type=jnp.float32).reshape(D, 3, width_all)
        grad_attn_in = jnp.dot(grad_proj, qkv_flat.T, preferred_element_type=jnp.float32)
        grad_gain_one = lax.optimization_barrier(jnp.sum(grad_attn_in * normed_one, axis=0))
        grad_input = (grad_mid + norm_back(grad_attn_in * norm1_gain, normed_one, spread_one)).astype(jnp.bfloat16)
        sums_one, sums_wqkv, sums_wo, sums_two, sums_w1, sums_w2 = carry
        carry = (sums_one + grad_gain_one, sums_wqkv + grad_wqkv, sums_wo + grad_wo, sums_two + grad_gain_two, sums_w1 + grad_w1, sums_w2 + grad_w2)
        return (carry, (result, grad_input))
    start = (jnp.zeros((D,), jnp.float32), jnp.zeros((D, 3, width_all), jnp.float32), jnp.zeros((width_all, D), jnp.float32), jnp.zeros((D,), jnp.float32), jnp.zeros((D, 2, FF), jnp.float32), jnp.zeros((FF, D), jnp.float32))
    inputs = (tokens.reshape(SEQS, SEQ_LEN, D), segment_ids.reshape(SEQS, SEQ_LEN), positions.reshape(SEQS, SEQ_LEN), cotangent.reshape(SEQS, SEQ_LEN, D))
    finals, stacked = lax.scan(one_sequence, start, inputs)
    output = stacked[0].reshape(TOKENS, D)
    input_grad = stacked[1].reshape(TOKENS, D)
    return (output, input_grad, finals[0], finals[1], finals[2], finals[3], finals[4], finals[5])
```

```python
import functools
import math

import jax
import jax.numpy as jnp
from jax import lax
from jax.sharding import PartitionSpec as P

HEAD_DIM = 64
SEQ_LEN = 512


EPS = 1e-05
THETA = 160000.0
NEG_FILL = -1e30
INV_ROOT_TWO_PI = 0.3989422804014327


def norm_rows(rows):
    centered = rows - jnp.mean(rows, axis=-1, keepdims=True)
    inv_spread = lax.rsqrt(jnp.mean(centered * centered, axis=-1, keepdims=True) + EPS)
    return (centered * inv_spread, inv_spread)


def norm_back(grad_rows, normed, inv_spread):
    return inv_spread * (
        grad_rows
        - jnp.mean(grad_rows, axis=-1, keepdims=True)
        - normed * jnp.mean(grad_rows * normed, axis=-1, keepdims=True)
    )


def rope_tables(position_ids):
    half_dim = HEAD_DIM // 2
    freqs = jnp.exp(-math.log(THETA) * (jnp.arange(half_dim, dtype=jnp.float32) * 2.0 / HEAD_DIM))
    angles = position_ids.astype(jnp.float32)[:, None] * freqs[None, :]
    cos_table = jnp.concatenate([jnp.cos(angles), jnp.cos(angles)], axis=-1)[:, None, :]
    sin_table = jnp.concatenate([jnp.sin(angles), jnp.sin(angles)], axis=-1)[:, None, :]
    return (cos_table, sin_table)


def rotate(values, cos_table, sin_table):
    half_dim = HEAD_DIM // 2
    turned = jnp.concatenate([-values[..., half_dim:], values[..., :half_dim]], axis=-1)
    return values * cos_table + turned * sin_table


def unrotate(grads, cos_table, sin_table):
    half_dim = HEAD_DIM // 2
    weighted = grads * sin_table
    turned = jnp.concatenate([weighted[..., half_dim:], -weighted[..., :half_dim]], axis=-1)
    return grads * cos_table + turned


def attend(query, key_rot, value, seg_row):
    scale = HEAD_DIM ** (-0.5)
    scores = jnp.einsum("qhd,khd->hqk", query, key_rot, preferred_element_type=jnp.float32) * scale
    allowed = (seg_row[:, None] == seg_row[None, :])[None]
    scores = jnp.where(allowed, scores, NEG_FILL)
    row_max = jnp.max(scores, axis=-1)
    expd = jnp.exp(scores - row_max[..., None])
    total = jnp.sum(expd, axis=-1)
    log_total = row_max + jnp.log(total)
    probs = (expd / total[..., None]).astype(jnp.bfloat16)
    attended = jnp.einsum("hqk,khd->qhd", probs, value, preferred_element_type=jnp.float32)
    return (attended.astype(jnp.bfloat16), log_total)


def attend_back(query, key_rot, value, attended, grad_out, log_total, seg_row):
    scale = HEAD_DIM ** (-0.5)
    scores = jnp.einsum("qhd,khd->hqk", query, key_rot, preferred_element_type=jnp.float32) * scale
    allowed = (seg_row[:, None] == seg_row[None, :])[None]
    probs = jnp.where(allowed, jnp.exp(scores - log_total[..., None]), 0.0)
    probs_low = probs.astype(jnp.bfloat16)
    grad_value = jnp.einsum("hqk,qhd->khd", probs_low, grad_out, preferred_element_type=jnp.float32)
    grad_probs = jnp.einsum("qhd,khd->hqk", grad_out, value, preferred_element_type=jnp.float32)
    delta = jnp.sum(grad_out.astype(jnp.float32) * attended.astype(jnp.float32), axis=-1).T
    grad_scores = (probs * (grad_probs - delta[..., None]) * scale).astype(jnp.bfloat16)
    grad_query = jnp.einsum(
        "hqk,khd->qhd", grad_scores, key_rot, preferred_element_type=jnp.float32
    )
    grad_key = jnp.einsum("hqk,qhd->khd", grad_scores, query, preferred_element_type=jnp.float32)
    return (grad_query, grad_key, grad_value)


def contract_rows(left, right):
    return lax.dot_general(
        left, right, (((0,), (0,)), ((), ())), preferred_element_type=jnp.float32
    )


def contract_cols(left, right):
    return lax.dot_general(
        left, right, (((1,), (1,)), ((), ())), preferred_element_type=jnp.float32
    )


def swap(array, axis, size, bit):
    return lax.ppermute(array, axis, [(i, i ^ bit) for i in range(size)])


def half_of(array, dim, which):
    length = array.shape[dim] // 2
    return lax.dynamic_slice_in_dim(array, which * length, length, dim)


def sum_over(array, axis, size, plan):
    me = lax.axis_index(axis)
    for bit, dim in plan:
        mine = jnp.where((me & bit) != 0, 1, 0)
        arrived = swap(half_of(array, dim, 1 - mine), axis, size, bit)
        array = (
            half_of(array, dim, mine).astype(jnp.float32) + arrived.astype(jnp.float32)
        ).astype(jnp.bfloat16)
    for bit, dim in reversed(plan):
        arrived = swap(array, axis, size, bit)
        upper = (me & bit) != 0
        first = jnp.where(upper, arrived, array)
        second = jnp.where(upper, array, arrived)
        array = jnp.concatenate([first, second], axis=dim)
    return array


def per_device(
    dp_size,
    tp_size,
    tokens,
    segment_ids,
    positions,
    norm1_gain,
    qkv_weight,
    out_weight,
    norm2_gain,
    mlp_in_weight,
    mlp_out_weight,
    cotangent,
):
    local_len = segment_ids.shape[0]
    seq_count = local_len // SEQ_LEN
    head_width = out_weight.shape[0]
    head_count = head_width // HEAD_DIM
    own = tokens.shape[0]
    paired = tp_size == 2 and seq_count == 1
    if paired:
        upper = lax.axis_index("tensor") != 0

        def own_first(array):
            return jnp.where(upper, jnp.concatenate([array[own:], array[:own]]), array)

        segment_ids = own_first(segment_ids)
        positions = own_first(positions)

    def gather(rows):
        if paired:
            return jnp.concatenate([rows, swap(rows, "tensor", 2, 1)], axis=0)
        return lax.all_gather(rows, "tensor", axis=0, tiled=True)

    def scatter_sum(product, rows):
        if paired:
            other = swap(product(rows[own:]).astype(jnp.bfloat16), "tensor", 2, 1)
            return product(rows[:own]) + other.astype(jnp.float32)
        return lax.psum_scatter(product(rows), "tensor", scatter_dimension=0, tiled=True)

    bits = [1 << b for b in range(dp_size.bit_length() - 1)]
    power = dp_size == 1 << len(bits) and dp_size >= 4
    orders = (bits, bits[1::-1] + bits[2:])

    def total(array, dims, order):
        if power:
            plan = [(bit, dims[min(i, len(dims) - 1)]) for i, bit in enumerate(orders[order])]
            return sum_over(array.astype(jnp.bfloat16), "dp", dp_size, plan)
        return lax.psum(array.astype(jnp.bfloat16), "dp")

    def split_seq(array):
        return array.reshape((seq_count, SEQ_LEN) + array.shape[1:])

    full_cot = gather(cotangent)
    token_f32 = tokens.astype(jnp.float32)
    normed_one, spread_one = norm_rows(token_f32)
    attn_in = (normed_one * norm1_gain).astype(jnp.bfloat16)
    full_one = gather(attn_in)
    projected = [
        jnp.dot(full_one, qkv_weight[:, c], preferred_element_type=jnp.float32) for c in range(3)
    ]
    cos_table, sin_table = rope_tables(positions)
    query = rotate(
        projected[0].reshape(local_len, head_count, HEAD_DIM), cos_table, sin_table
    ).astype(jnp.bfloat16)
    key_rot = rotate(
        projected[1].reshape(local_len, head_count, HEAD_DIM), cos_table, sin_table
    ).astype(jnp.bfloat16)
    value = projected[2].reshape(local_len, head_count, HEAD_DIM).astype(jnp.bfloat16)

    def attend_item(item):
        return attend(item[0], item[1], item[2], item[3])

    attended, log_total = lax.map(
        attend_item,
        (split_seq(query), split_seq(key_rot), split_seq(value), split_seq(segment_ids)),
    )
    attended = attended.reshape(local_len, head_count, HEAD_DIM)
    attn_flat = attended.reshape(local_len, head_width)
    resid_mid = token_f32 + scatter_sum(
        lambda rows: jnp.dot(rows, out_weight, preferred_element_type=jnp.float32), attn_flat
    )
    normed_two, spread_two = norm_rows(resid_mid)
    mlp_in = (normed_two * norm2_gain).astype(jnp.bfloat16)
    full_two = gather(mlp_in)
    gate_pre = jnp.dot(full_two, mlp_in_weight[:, 0], preferred_element_type=jnp.float32)
    up_part = jnp.dot(full_two, mlp_in_weight[:, 1], preferred_element_type=jnp.float32)
    cdf = 0.5 * (1.0 + jax.scipy.special.erf(gate_pre * (1.0 / math.sqrt(2.0))))
    activated = gate_pre * cdf
    hidden = (activated * up_part).astype(jnp.bfloat16)

    grad_w2 = contract_rows(hidden, full_cot).astype(jnp.bfloat16)
    columns = grad_w2.shape[1] // 2
    grad_w2 = [
        total(grad_w2[:, i * columns : (i + 1) * columns], (1, 1, 0), i) for i in range(2)
    ]
    grad_w2 = jnp.concatenate(grad_w2, axis=1).astype(jnp.float32)

    grad_hidden = contract_cols(full_cot, mlp_out_weight)
    slope = cdf + gate_pre * jnp.exp(-0.5 * gate_pre * gate_pre) * INV_ROOT_TWO_PI
    grad_gate = (grad_hidden * up_part * slope).astype(jnp.bfloat16)
    grad_up = (grad_hidden * activated).astype(jnp.bfloat16)
    grad_w1 = jnp.stack(
        [
            total(contract_rows(grad_gate, full_two), (1, 1, 1, 0), 0),
            total(contract_rows(grad_up, full_two), (1, 1, 1, 0), 1),
        ]
    )
    grad_w1 = grad_w1.transpose(2, 0, 1).astype(jnp.float32)
    output = (
        resid_mid
        + scatter_sum(
            lambda rows: jnp.dot(rows, mlp_out_weight, preferred_element_type=jnp.float32), hidden
        )
    ).astype(jnp.bfloat16)
    grad_gu = jnp.concatenate([grad_gate, grad_up], axis=1)

    def back_mlp(rows):
        width = grad_gate.shape[1]
        return contract_cols(rows[:, :width], mlp_in_weight[:, 0]) + contract_cols(
            rows[:, width:], mlp_in_weight[:, 1]
        )

    grad_mlp_in = scatter_sum(back_mlp, grad_gu)
    grad_gain_two = jnp.sum(grad_mlp_in * normed_two, axis=0)
    grad_mid = cotangent.astype(jnp.float32) + norm_back(
        grad_mlp_in * norm2_gain, normed_two, spread_two
    )
    full_mid = gather(grad_mid.astype(jnp.bfloat16))
    grad_wo = contract_rows(attn_flat, full_mid).astype(jnp.bfloat16)
    half_rows = grad_wo.shape[0] // 2
    grad_wo = jnp.concatenate(
        [total(grad_wo[i * half_rows : (i + 1) * half_rows], (0,), i) for i in range(2)], axis=0
    ).astype(jnp.float32)
    grad_att = (
        contract_cols(full_mid, out_weight)
        .astype(jnp.bfloat16)
        .reshape(local_len, head_count, HEAD_DIM)
    )

    def back_item(item):
        return attend_back(item[0], item[1], item[2], item[3], item[4], item[5], item[6])

    grad_query, grad_key, grad_value = lax.map(
        back_item,
        (
            split_seq(query),
            split_seq(key_rot),
            split_seq(value),
            split_seq(attended),
            split_seq(grad_att),
            log_total,
            split_seq(segment_ids),
        ),
    )
    grad_query = grad_query.reshape(local_len, head_count, HEAD_DIM)
    grad_key = grad_key.reshape(local_len, head_count, HEAD_DIM)
    grad_proj = jnp.concatenate(
        [
            unrotate(grad_query, cos_table, sin_table).reshape(local_len, head_width),
            unrotate(grad_key, cos_table, sin_table).reshape(local_len, head_width),
            grad_value.reshape(local_len, head_width),
        ],
        axis=1,
    ).astype(jnp.bfloat16)
    grad_wqkv = jnp.concatenate(
        [
            contract_rows(full_one, grad_proj[:, c * head_width : (c + 1) * head_width])
            for c in range(3)
        ],
        axis=0,
    ).astype(jnp.bfloat16)
    half_rows = grad_wqkv.shape[0] // 2
    grad_wqkv = jnp.concatenate(
        [total(grad_wqkv[i * half_rows : (i + 1) * half_rows], (0,), i) for i in range(2)], axis=0
    )
    grad_wqkv = grad_wqkv.reshape(3, -1, head_width).transpose(1, 0, 2).astype(jnp.float32)

    def back_qkv(rows):
        return sum(
            contract_cols(rows[:, c * head_width : (c + 1) * head_width], qkv_weight[:, c])
            for c in range(3)
        )

    grad_attn_in = scatter_sum(back_qkv, grad_proj)
    grad_gain_one = jnp.sum(grad_attn_in * normed_one, axis=0)
    input_grad = (grad_mid + norm_back(grad_attn_in * norm1_gain, normed_one, spread_one)).astype(
        jnp.bfloat16
    )
    gains = jnp.stack([grad_gain_one, grad_gain_two])
    if power and tp_size == 2:
        gains = gains + swap(gains, "tensor", 2, 1)
        for bit in bits:
            gains = gains + swap(gains, "dp", dp_size, bit)
    else:
        gains = lax.psum(gains, ("dp", "tensor"))
    return (output, input_grad, gains[0], grad_wqkv, grad_wo, gains[1], grad_w1, grad_w2)


def solution(mesh):
    body = functools.partial(per_device, mesh.shape["dp"], mesh.shape["tensor"])
    return jax.shard_map(
        body,
        mesh=mesh,
        in_specs=(
            P(("dp", "tensor"), None),
            P("dp"),
            P("dp"),
            P(),
            P(None, None, "tensor"),
            P("tensor", None),
            P(),
            P(None, None, "tensor"),
            P("tensor", None),
            P(("dp", "tensor"), None),
        ),
        out_specs=(
            P(("dp", "tensor"), None),
            P(("dp", "tensor"), None),
            P(),
            P(None, None, "tensor"),
            P("tensor", None),
            P(),
            P(None, None, "tensor"),
            P("tensor", None),
        ),
        check_vma=False,
    )
```

```python
import functools
import math

import jax
import jax.numpy as jnp
from jax import lax
from jax.experimental import pallas as pl
from jax.experimental.pallas import tpu as pltpu
from jax.sharding import PartitionSpec as P

HEAD_DIM = 64
SEQ_LEN = 512


EPS = 1e-05
THETA = 160000.0
NEG_FILL = -1e30
INV_ROOT_TWO_PI = 0.3989422804014327


def norm_rows(rows):
    centered = rows - jnp.mean(rows, axis=-1, keepdims=True)
    inv_spread = lax.rsqrt(jnp.mean(centered * centered, axis=-1, keepdims=True) + EPS)
    return (centered * inv_spread, inv_spread)


def norm_back(grad_rows, normed, inv_spread):
    return inv_spread * (
        grad_rows
        - jnp.mean(grad_rows, axis=-1, keepdims=True)
        - normed * jnp.mean(grad_rows * normed, axis=-1, keepdims=True)
    )


def rope_tables(position_ids):
    half_dim = HEAD_DIM // 2
    freqs = jnp.exp(-math.log(THETA) * (jnp.arange(half_dim, dtype=jnp.float32) * 2.0 / HEAD_DIM))
    angles = position_ids.astype(jnp.float32)[:, None] * freqs[None, :]
    cos_table = jnp.concatenate([jnp.cos(angles), jnp.cos(angles)], axis=-1)[:, None, :]
    sin_table = jnp.concatenate([jnp.sin(angles), jnp.sin(angles)], axis=-1)[:, None, :]
    return (cos_table, sin_table)


def rotate(values, cos_table, sin_table):
    half_dim = HEAD_DIM // 2
    turned = jnp.concatenate([-values[..., half_dim:], values[..., :half_dim]], axis=-1)
    return values * cos_table + turned * sin_table


def unrotate(grads, cos_table, sin_table):
    half_dim = HEAD_DIM // 2
    weighted = grads * sin_table
    turned = jnp.concatenate([weighted[..., half_dim:], -weighted[..., :half_dim]], axis=-1)
    return grads * cos_table + turned


def attend(query, key_rot, value, seg_row):
    scale = HEAD_DIM ** (-0.5)
    scores = jnp.einsum("qhd,khd->hqk", query, key_rot, preferred_element_type=jnp.float32) * scale
    allowed = (seg_row[:, None] == seg_row[None, :])[None]
    scores = jnp.where(allowed, scores, NEG_FILL)
    row_max = jnp.max(scores, axis=-1)
    expd = jnp.exp(scores - row_max[..., None])
    total = jnp.sum(expd, axis=-1)
    log_total = row_max + jnp.log(total)
    probs = (expd / total[..., None]).astype(jnp.bfloat16)
    attended = jnp.einsum("hqk,khd->qhd", probs, value, preferred_element_type=jnp.float32)
    return (attended.astype(jnp.bfloat16), log_total)


def attend_back(query, key_rot, value, attended, grad_out, log_total, seg_row):
    scale = HEAD_DIM ** (-0.5)
    scores = jnp.einsum("qhd,khd->hqk", query, key_rot, preferred_element_type=jnp.float32) * scale
    allowed = (seg_row[:, None] == seg_row[None, :])[None]
    probs = jnp.where(allowed, jnp.exp(scores - log_total[..., None]), 0.0)
    probs_low = probs.astype(jnp.bfloat16)
    grad_value = jnp.einsum("hqk,qhd->khd", probs_low, grad_out, preferred_element_type=jnp.float32)
    grad_probs = jnp.einsum("qhd,khd->hqk", grad_out, value, preferred_element_type=jnp.float32)
    delta = jnp.sum(grad_out.astype(jnp.float32) * attended.astype(jnp.float32), axis=-1).T
    grad_scores = (probs * (grad_probs - delta[..., None]) * scale).astype(jnp.bfloat16)
    grad_query = jnp.einsum(
        "hqk,khd->qhd", grad_scores, key_rot, preferred_element_type=jnp.float32
    )
    grad_key = jnp.einsum("hqk,qhd->khd", grad_scores, query, preferred_element_type=jnp.float32)
    return (grad_query, grad_key, grad_value)


def contract_rows(left, right):
    return lax.dot_general(
        left, right, (((0,), (0,)), ((), ())), preferred_element_type=jnp.float32
    )


def contract_cols(left, right):
    return lax.dot_general(
        left, right, (((1,), (1,)), ((), ())), preferred_element_type=jnp.float32
    )


def swap(array, axis, size, bit):
    return lax.ppermute(array, axis, [(i, i ^ bit) for i in range(size)])


def half_of(array, dim, which):
    length = array.shape[dim] // 2
    return lax.dynamic_slice_in_dim(array, which * length, length, dim)


def halve(array, axis, size, bit, dim):
    mine = (lax.axis_index(axis) // bit) % 2
    arrived = swap(half_of(array, dim, 1 - mine), axis, size, bit)
    return half_of(array, dim, mine), arrived


def add_halves(kept, arrived):
    return (kept.astype(jnp.float32) + arrived.astype(jnp.float32)).astype(jnp.bfloat16)


def sum_over(array, axis, size, plan):
    me = lax.axis_index(axis)
    for bit, dim in plan:
        array = add_halves(*halve(array, axis, size, bit, dim))
    for bit, dim in reversed(plan):
        arrived = swap(array, axis, size, bit)
        upper = (me & bit) != 0
        first = jnp.where(upper, arrived, array)
        second = jnp.where(upper, array, arrived)
        array = jnp.concatenate([first, second], axis=dim)
    return array


def shrink(shape, dim):
    return tuple(n // 2 if d == dim else n for d, n in enumerate(shape))


def sum_kernel(axis, plans, done, *refs):
    count = len(plans)
    sources, outs = refs[:count], refs[count : 2 * count]
    rest = refs[2 * count :]
    send_sem, recv_sem = rest[-2:]
    landed = []
    at = 0
    for plan, skip in zip(plans, done):
        landed.append([None] * skip + list(rest[at : at + len(plan) - skip]))
        at += len(plan) - skip
    steps = len(plans[0])
    me = lax.axis_index(axis)
    side = {bit: (me // bit) % 2 for bit, _ in plans[0]}

    barrier = pltpu.get_barrier_semaphore()
    for bit in side:
        pl.semaphore_signal(
            barrier,
            inc=1,
            device_id={axis: me + bit - 2 * bit * side[bit]},
            device_id_type=pl.DeviceIdType.MESH,
        )
    pl.semaphore_wait(barrier, len(side))

    slot = iter(range(10000))

    def send(src, dst, bit):
        i = next(slot)
        copy = pltpu.make_async_remote_copy(
            src_ref=src,
            dst_ref=dst,
            send_sem=send_sem.at[i],
            recv_sem=recv_sem.at[i],
            device_id={axis: me + bit - 2 * bit * side[bit]},
            device_id_type=pl.DeviceIdType.MESH,
        )
        copy.start()
        return copy

    def part(ref, dim, which):
        length = ref.shape[dim] // 2
        start = pl.multiple_of(which * length, length)
        if dim == 0:
            return ref.at[pl.ds(start, length), :]
        return ref.at[:, pl.ds(start, length)]

    def add(dst, left, right):
        rows = dst.shape[0]
        chunk = 16

        @pl.loop(0, rows // chunk)
        def _(i):
            span = pl.ds(pl.multiple_of(i * chunk, chunk), chunk)
            dst[span, :] = (
                left[span, :].astype(jnp.float32) + right[span, :].astype(jnp.float32)
            ).astype(jnp.bfloat16)

    def region(s, level):
        starts = [0, 0]
        sizes = list(outs[s].shape)
        for bit, dim in plans[s][:level]:
            sizes[dim] //= 2
            starts[dim] = starts[dim] + side[bit] * sizes[dim]
        index = tuple(
            pl.ds(start if isinstance(start, int) else pl.multiple_of(start, size), size)
            for start, size in zip(starts, sizes)
        )
        return outs[s].at[index]

    copies = []
    current = list(sources)
    flying = [None] * count
    for step in range(min(done), steps + 1):
        for s in range(count):
            if step > done[s]:
                bit, dim = plans[s][step - 1]
                flying[s].wait_recv()
                got = landed[s][step - 1]
                target = got if step < steps else region(s, steps)
                add(target, part(current[s], dim, side[bit]), got)
                current[s] = got
            if done[s] <= step < steps:
                bit, dim = plans[s][step]
                flying[s] = send(part(current[s], dim, 1 - side[bit]), landed[s][step], bit)
                copies.append(flying[s])
            if step == steps:
                bit, _ = plans[s][steps - 1]
                flying[s] = send(region(s, steps), region(s, steps), bit)
                copies.append(flying[s])
    for step in reversed(range(steps - 1)):
        for s in range(count):
            flying[s].wait_recv()
            bit, _ = plans[s][step]
            flying[s] = send(region(s, step + 1), region(s, step + 1), bit)
            copies.append(flying[s])
    for s in range(count):
        flying[s].wait_recv()
    for copy in copies:
        copy.wait_send()


def kernel_sums(axis, arrays, plans, done):
    shapes, scratch = [], []
    for array, plan, skip in zip(arrays, plans, done):
        shape = list(array.shape)
        for _, dim in plan[:skip]:
            shape[dim] *= 2
        shapes.append(tuple(shape))
        piece = array.shape
        for _, dim in plan[skip:]:
            piece = shrink(piece, dim)
            scratch.append(pltpu.VMEM(piece, jnp.bfloat16))
    copies = sum(2 * len(plan) - skip for plan, skip in zip(plans, done))
    return pl.pallas_call(
        functools.partial(sum_kernel, axis, plans, done),
        out_shape=[jax.ShapeDtypeStruct(shape, jnp.bfloat16) for shape in shapes],
        in_specs=[pl.BlockSpec(memory_space=pltpu.VMEM)] * len(arrays),
        out_specs=[pl.BlockSpec(memory_space=pltpu.VMEM)] * len(arrays),
        scratch_shapes=scratch
        + [pltpu.SemaphoreType.DMA((copies,)), pltpu.SemaphoreType.DMA((copies,))],
        compiler_params=pltpu.CompilerParams(
            collective_id=0, has_side_effects=True, vmem_limit_bytes=60 * 1024 * 1024
        ),
        name="sum_grads",
    )(*arrays)


def fits(shape, plan):
    for _, dim in plan:
        if shape[dim] % 2:
            return False
        shape = shrink(shape, dim)
    return shape[0] % 16 == 0 and shape[1] % 128 == 0


def per_device(
    dp_size,
    tp_size,
    tokens,
    segment_ids,
    positions,
    norm1_gain,
    qkv_weight,
    out_weight,
    norm2_gain,
    mlp_in_weight,
    mlp_out_weight,
    cotangent,
):
    local_len = segment_ids.shape[0]
    seq_count = local_len // SEQ_LEN
    head_width = out_weight.shape[0]
    head_count = head_width // HEAD_DIM
    own = tokens.shape[0]
    paired = tp_size == 2 and seq_count == 1
    if paired:
        upper = lax.axis_index("tensor") != 0

        def own_first(array):
            return jnp.where(upper, jnp.concatenate([array[own:], array[:own]]), array)

        segment_ids = own_first(segment_ids)
        positions = own_first(positions)

    def gather(rows):
        if paired:
            return jnp.concatenate([rows, swap(rows, "tensor", 2, 1)], axis=0)
        return lax.all_gather(rows, "tensor", axis=0, tiled=True)

    def scatter_sum(product, rows):
        if paired:
            other = swap(product(rows[own:]).astype(jnp.bfloat16), "tensor", 2, 1)
            return product(rows[:own]) + other.astype(jnp.float32)
        return lax.psum_scatter(product(rows), "tensor", scatter_dimension=0, tiled=True)

    bits = [1 << b for b in range(dp_size.bit_length() - 1)]
    power = dp_size == 1 << len(bits) and dp_size >= 4
    wide = (mlp_out_weight.shape[0], tokens.shape[1])
    tall = (qkv_weight.shape[1] * tokens.shape[1] // 2, head_width)
    flat = (head_width // 2, tokens.shape[1])
    orders = (bits, bits[1::-1] + bits[2:], bits[2:3] + bits[:2] + bits[3:])

    def plan_of(order, dims):
        return tuple((bit, dims[min(i, len(dims) - 1)]) for i, bit in enumerate(orders[order]))

    wide_plans = [plan_of(order, (1, 1, 1, 0)) for order in range(3)]
    row_plans = [plan_of(order, (0,)) for order in range(2)]
    kernel_way = (
        power
        and all(fits(wide, plan) for plan in wide_plans)
        and all(fits(tall, plan) and fits(flat, plan) for plan in row_plans)
    )
    early = 2

    def total(array, plan):
        if power:
            return sum_over(array, "dp", dp_size, plan)
        return lax.psum(array, "dp")

    def split_seq(array):
        return array.reshape((seq_count, SEQ_LEN) + array.shape[1:])

    full_cot = gather(cotangent)
    token_f32 = tokens.astype(jnp.float32)
    normed_one, spread_one = norm_rows(token_f32)
    attn_in = (normed_one * norm1_gain).astype(jnp.bfloat16)
    full_one = gather(attn_in)
    projected = [
        jnp.dot(full_one, qkv_weight[:, c], preferred_element_type=jnp.float32) for c in range(3)
    ]
    cos_table, sin_table = rope_tables(positions)
    query = rotate(
        projected[0].reshape(local_len, head_count, HEAD_DIM), cos_table, sin_table
    ).astype(jnp.bfloat16)
    key_rot = rotate(
        projected[1].reshape(local_len, head_count, HEAD_DIM), cos_table, sin_table
    ).astype(jnp.bfloat16)
    value = projected[2].reshape(local_len, head_count, HEAD_DIM).astype(jnp.bfloat16)

    def attend_item(item):
        return attend(item[0], item[1], item[2], item[3])

    attended, log_total = lax.map(
        attend_item,
        (split_seq(query), split_seq(key_rot), split_seq(value), split_seq(segment_ids)),
    )
    attended = attended.reshape(local_len, head_count, HEAD_DIM)
    attn_flat = attended.reshape(local_len, head_width)
    resid_mid = token_f32 + scatter_sum(
        lambda rows: jnp.dot(rows, out_weight, preferred_element_type=jnp.float32), attn_flat
    )
    normed_two, spread_two = norm_rows(resid_mid)
    mlp_in = (normed_two * norm2_gain).astype(jnp.bfloat16)
    full_two = gather(mlp_in)
    gate_pre = jnp.dot(full_two, mlp_in_weight[:, 0], preferred_element_type=jnp.float32)
    up_part = jnp.dot(full_two, mlp_in_weight[:, 1], preferred_element_type=jnp.float32)
    cdf = 0.5 * (1.0 + jax.scipy.special.erf(gate_pre * (1.0 / math.sqrt(2.0))))
    activated = gate_pre * cdf
    hidden = (activated * up_part).astype(jnp.bfloat16)

    grad_w2 = contract_rows(hidden, full_cot).astype(jnp.bfloat16)
    grad_hidden = contract_cols(full_cot, mlp_out_weight)
    slope = cdf + gate_pre * jnp.exp(-0.5 * gate_pre * gate_pre) * INV_ROOT_TWO_PI
    grad_gate = (grad_hidden * up_part * slope).astype(jnp.bfloat16)
    grad_up = (grad_hidden * activated).astype(jnp.bfloat16)
    wide_grads = [
        grad_w2,
        contract_rows(grad_gate, full_two).astype(jnp.bfloat16),
        contract_rows(grad_up, full_two).astype(jnp.bfloat16),
    ]
    if kernel_way:
        pending = [
            halve(grad, "dp", dp_size, *plan[0]) for grad, plan in zip(wide_grads, wide_plans)
        ]
    output = (
        resid_mid
        + scatter_sum(
            lambda rows: jnp.dot(rows, mlp_out_weight, preferred_element_type=jnp.float32), hidden
        )
    ).astype(jnp.bfloat16)
    grad_gu = jnp.concatenate([grad_gate, grad_up], axis=1)

    def back_mlp(rows):
        width = grad_gate.shape[1]
        return contract_cols(rows[:, :width], mlp_in_weight[:, 0]) + contract_cols(
            rows[:, width:], mlp_in_weight[:, 1]
        )

    grad_mlp_in = scatter_sum(back_mlp, grad_gu)
    grad_gain_two = jnp.sum(grad_mlp_in * normed_two, axis=0)
    grad_mid = cotangent.astype(jnp.float32) + norm_back(
        grad_mlp_in * norm2_gain, normed_two, spread_two
    )
    full_mid = gather(grad_mid.astype(jnp.bfloat16))
    grad_wo = contract_rows(attn_flat, full_mid).astype(jnp.bfloat16)
    grad_att = contract_cols(full_mid, out_weight).astype(jnp.bfloat16)
    if kernel_way:
        pending, grad_att = lax.optimization_barrier((pending, grad_att))
        pending = [
            halve(add_halves(*pair), "dp", dp_size, *plan[1])
            for pair, plan in zip(pending, wide_plans)
        ]
    grad_att = grad_att.reshape(local_len, head_count, HEAD_DIM)

    def back_item(item):
        return attend_back(item[0], item[1], item[2], item[3], item[4], item[5], item[6])

    grad_query, grad_key, grad_value = lax.map(
        back_item,
        (
            split_seq(query),
            split_seq(key_rot),
            split_seq(value),
            split_seq(attended),
            split_seq(grad_att),
            log_total,
            split_seq(segment_ids),
        ),
    )
    grad_query = grad_query.reshape(local_len, head_count, HEAD_DIM)
    grad_key = grad_key.reshape(local_len, head_count, HEAD_DIM)
    grad_proj = jnp.concatenate(
        [
            unrotate(grad_query, cos_table, sin_table).reshape(local_len, head_width),
            unrotate(grad_key, cos_table, sin_table).reshape(local_len, head_width),
            grad_value.reshape(local_len, head_width),
        ],
        axis=1,
    ).astype(jnp.bfloat16)
    grad_wqkv = jnp.concatenate(
        [
            contract_rows(full_one, grad_proj[:, c * head_width : (c + 1) * head_width])
            for c in range(3)
        ],
        axis=0,
    ).astype(jnp.bfloat16)
    def back_qkv(rows):
        return sum(
            contract_cols(rows[:, c * head_width : (c + 1) * head_width], qkv_weight[:, c])
            for c in range(3)
        )

    grad_attn_in = scatter_sum(back_qkv, grad_proj)
    grad_gain_one = jnp.sum(grad_attn_in * normed_one, axis=0)
    input_grad = (grad_mid + norm_back(grad_attn_in * norm1_gain, normed_one, spread_one)).astype(
        jnp.bfloat16
    )
    row_grads = [
        grad_wo[: flat[0]],
        grad_wo[flat[0] :],
        grad_wqkv[: tall[0]],
        grad_wqkv[tall[0] :],
    ]
    plans = wide_plans + [row_plans[0], row_plans[1]] * 2
    if kernel_way:
        parts = [add_halves(*pair) for pair in pending] + row_grads
        sums = kernel_sums("dp", parts, plans, [early] * 3 + [0] * 4)
    else:
        sums = [total(grad, plan) for grad, plan in zip(wide_grads + row_grads, plans)]
    grad_w2 = sums[0].astype(jnp.float32)
    grad_w1 = jnp.stack(sums[1:3]).transpose(2, 0, 1).astype(jnp.float32)
    grad_wo = jnp.concatenate(sums[3:5], axis=0).astype(jnp.float32)
    grad_wqkv = jnp.concatenate(sums[5:7], axis=0).reshape(3, -1, head_width)
    grad_wqkv = grad_wqkv.transpose(1, 0, 2).astype(jnp.float32)
    gains = jnp.stack([grad_gain_one, grad_gain_two])
    if power and tp_size == 2:
        gains = gains + swap(gains, "tensor", 2, 1)
        for bit in bits:
            gains = gains + swap(gains, "dp", dp_size, bit)
    else:
        gains = lax.psum(gains, ("dp", "tensor"))
    return (output, input_grad, gains[0], grad_wqkv, grad_wo, gains[1], grad_w1, grad_w2)


def solution(mesh):
    body = functools.partial(per_device, mesh.shape["dp"], mesh.shape["tensor"])
    return jax.shard_map(
        body,
        mesh=mesh,
        in_specs=(
            P(("dp", "tensor"), None),
            P("dp"),
            P("dp"),
            P(),
            P(None, None, "tensor"),
            P("tensor", None),
            P(),
            P(None, None, "tensor"),
            P("tensor", None),
            P(("dp", "tensor"), None),
        ),
        out_specs=(
            P(("dp", "tensor"), None),
            P(("dp", "tensor"), None),
            P(),
            P(None, None, "tensor"),
            P("tensor", None),
            P(),
            P(None, None, "tensor"),
            P("tensor", None),
        ),
        check_vma=False,
    )
```

```python
import functools
import math

import jax
import jax.numpy as jnp
from jax import lax
from jax.experimental import pallas as pl
from jax.experimental.pallas import tpu as pltpu
from jax.sharding import PartitionSpec as P

HEAD_DIM = 64
SEQ_LEN = 512


EPS = 1e-05
THETA = 160000.0
NEG_FILL = -1e30
INV_ROOT_TWO_PI = 0.3989422804014327


def norm_rows(rows):
    centered = rows - jnp.mean(rows, axis=-1, keepdims=True)
    inv_spread = lax.rsqrt(jnp.mean(centered * centered, axis=-1, keepdims=True) + EPS)
    return (centered * inv_spread, inv_spread)


def norm_back(grad_rows, normed, inv_spread):
    return inv_spread * (
        grad_rows
        - jnp.mean(grad_rows, axis=-1, keepdims=True)
        - normed * jnp.mean(grad_rows * normed, axis=-1, keepdims=True)
    )


def rope_tables(position_ids):
    half_dim = HEAD_DIM // 2
    freqs = jnp.exp(-math.log(THETA) * (jnp.arange(half_dim, dtype=jnp.float32) * 2.0 / HEAD_DIM))
    angles = position_ids.astype(jnp.float32)[:, None] * freqs[None, :]
    cos_table = jnp.concatenate([jnp.cos(angles), jnp.cos(angles)], axis=-1)[:, None, :]
    sin_table = jnp.concatenate([jnp.sin(angles), jnp.sin(angles)], axis=-1)[:, None, :]
    return (cos_table, sin_table)


def rotate(values, cos_table, sin_table):
    half_dim = HEAD_DIM // 2
    turned = jnp.concatenate([-values[..., half_dim:], values[..., :half_dim]], axis=-1)
    return values * cos_table + turned * sin_table


def unrotate(grads, cos_table, sin_table):
    half_dim = HEAD_DIM // 2
    weighted = grads * sin_table
    turned = jnp.concatenate([weighted[..., half_dim:], -weighted[..., :half_dim]], axis=-1)
    return grads * cos_table + turned


def attend(query, key_rot, value, seg_row):
    scale = HEAD_DIM ** (-0.5)
    scores = jnp.einsum("qhd,khd->hqk", query, key_rot, preferred_element_type=jnp.float32) * scale
    allowed = (seg_row[:, None] == seg_row[None, :])[None]
    scores = jnp.where(allowed, scores, NEG_FILL)
    row_max = jnp.max(scores, axis=-1)
    expd = jnp.exp(scores - row_max[..., None])
    total = jnp.sum(expd, axis=-1)
    log_total = row_max + jnp.log(total)
    probs = (expd / total[..., None]).astype(jnp.bfloat16)
    attended = jnp.einsum("hqk,khd->qhd", probs, value, preferred_element_type=jnp.float32)
    return (attended.astype(jnp.bfloat16), log_total)


def attend_back(query, key_rot, value, attended, grad_out, log_total, seg_row):
    scale = HEAD_DIM ** (-0.5)
    scores = jnp.einsum("qhd,khd->hqk", query, key_rot, preferred_element_type=jnp.float32) * scale
    allowed = (seg_row[:, None] == seg_row[None, :])[None]
    probs = jnp.where(allowed, jnp.exp(scores - log_total[..., None]), 0.0)
    probs_low = probs.astype(jnp.bfloat16)
    grad_value = jnp.einsum("hqk,qhd->khd", probs_low, grad_out, preferred_element_type=jnp.float32)
    grad_probs = jnp.einsum("qhd,khd->hqk", grad_out, value, preferred_element_type=jnp.float32)
    delta = jnp.sum(grad_out.astype(jnp.float32) * attended.astype(jnp.float32), axis=-1).T
    grad_scores = (probs * (grad_probs - delta[..., None]) * scale).astype(jnp.bfloat16)
    grad_query = jnp.einsum(
        "hqk,khd->qhd", grad_scores, key_rot, preferred_element_type=jnp.float32
    )
    grad_key = jnp.einsum("hqk,qhd->khd", grad_scores, query, preferred_element_type=jnp.float32)
    return (grad_query, grad_key, grad_value)


def contract_rows(left, right):
    return lax.dot_general(
        left, right, (((0,), (0,)), ((), ())), preferred_element_type=jnp.float32
    )


def contract_cols(left, right):
    return lax.dot_general(
        left, right, (((1,), (1,)), ((), ())), preferred_element_type=jnp.float32
    )


def swap(array, axis, size, bit):
    return lax.ppermute(array, axis, [(i, i ^ bit) for i in range(size)])


def half_of(array, dim, which):
    length = array.shape[dim] // 2
    return lax.dynamic_slice_in_dim(array, which * length, length, dim)


def halve(array, axis, size, bit, dim):
    mine = (lax.axis_index(axis) // bit) % 2
    arrived = swap(half_of(array, dim, 1 - mine), axis, size, bit)
    return half_of(array, dim, mine), arrived


def add_halves(kept, arrived):
    return (kept.astype(jnp.float32) + arrived.astype(jnp.float32)).astype(jnp.bfloat16)


def sum_over(array, axis, size, plan):
    me = lax.axis_index(axis)
    for bit, dim in plan:
        array = add_halves(*halve(array, axis, size, bit, dim))
    for bit, dim in reversed(plan):
        arrived = swap(array, axis, size, bit)
        upper = (me & bit) != 0
        first = jnp.where(upper, arrived, array)
        second = jnp.where(upper, array, arrived)
        array = jnp.concatenate([first, second], axis=dim)
    return array


def shrink(shape, dim):
    return tuple(n // 2 if d == dim else n for d, n in enumerate(shape))


def sum_kernel(axis, plans, done, *refs):
    count = len(plans)
    sources, outs = refs[:count], refs[count : 2 * count]
    rest = refs[2 * count :]
    send_sem, recv_sem = rest[-2:]
    landed = []
    at = 0
    for plan, skip in zip(plans, done):
        landed.append([None] * skip + list(rest[at : at + len(plan) - skip]))
        at += len(plan) - skip
    steps = len(plans[0])
    me = lax.axis_index(axis)
    side = {bit: (me // bit) % 2 for bit, _ in plans[0]}

    barrier = pltpu.get_barrier_semaphore()
    for bit in side:
        pl.semaphore_signal(
            barrier,
            inc=1,
            device_id={axis: me + bit - 2 * bit * side[bit]},
            device_id_type=pl.DeviceIdType.MESH,
        )
    pl.semaphore_wait(barrier, len(side))

    slot = iter(range(10000))

    def send(src, dst, bit):
        i = next(slot)
        copy = pltpu.make_async_remote_copy(
            src_ref=src,
            dst_ref=dst,
            send_sem=send_sem.at[i],
            recv_sem=recv_sem.at[i],
            device_id={axis: me + bit - 2 * bit * side[bit]},
            device_id_type=pl.DeviceIdType.MESH,
        )
        copy.start()
        return copy

    def part(ref, dim, which):
        length = ref.shape[dim] // 2
        start = pl.multiple_of(which * length, length)
        if dim == 0:
            return ref.at[pl.ds(start, length), :]
        return ref.at[:, pl.ds(start, length)]

    def add(dst, left, right):
        rows = dst.shape[0]
        chunk = min(16, rows)

        @pl.loop(0, rows // chunk)
        def _(i):
            span = pl.ds(pl.multiple_of(i * chunk, chunk), chunk)
            dst[span, :] = (
                left[span, :].astype(jnp.float32) + right[span, :].astype(jnp.float32)
            ).astype(dst.dtype)

    def region(s, level):
        starts = [0, 0]
        sizes = list(outs[s].shape)
        for bit, dim in plans[s][:level]:
            sizes[dim] //= 2
            starts[dim] = starts[dim] + side[bit] * sizes[dim]
        index = tuple(
            pl.ds(start if isinstance(start, int) else pl.multiple_of(start, size), size)
            for start, size in zip(starts, sizes)
        )
        return outs[s].at[index]

    copies = []
    current = list(sources)
    flying = [None] * count
    for turn in range(2 * steps + 1 - min(done)):
        for s in range(count):
            step = turn + done[s]
            if step > 2 * steps:
                continue
            if step > done[s]:
                flying[s].wait_recv()
            if done[s] < step <= steps:
                bit, dim = plans[s][step - 1]
                got = landed[s][step - 1]
                target = got if step < steps else region(s, steps)
                add(target, part(current[s], dim, side[bit]), got)
                current[s] = got
            if step < steps:
                bit, dim = plans[s][step]
                flying[s] = send(part(current[s], dim, 1 - side[bit]), landed[s][step], bit)
                copies.append(flying[s])
            elif step < 2 * steps:
                level = 2 * steps - step
                bit, _ = plans[s][level - 1]
                flying[s] = send(region(s, level), region(s, level), bit)
                copies.append(flying[s])
    for copy in copies:
        copy.wait_send()


def kernel_sums(axis, arrays, plans, done):
    shapes, scratch = [], []
    for array, plan, skip in zip(arrays, plans, done):
        shape = list(array.shape)
        for _, dim in plan[:skip]:
            shape[dim] *= 2
        shapes.append(tuple(shape))
        piece = array.shape
        for _, dim in plan[skip:]:
            piece = shrink(piece, dim)
            scratch.append(pltpu.VMEM(piece, array.dtype))
    copies = sum(2 * len(plan) - skip for plan, skip in zip(plans, done))
    return pl.pallas_call(
        functools.partial(sum_kernel, axis, plans, done),
        out_shape=[
            jax.ShapeDtypeStruct(shape, array.dtype) for shape, array in zip(shapes, arrays)
        ],
        in_specs=[pl.BlockSpec(memory_space=pltpu.VMEM)] * len(arrays),
        out_specs=[pl.BlockSpec(memory_space=pltpu.VMEM)] * len(arrays),
        scratch_shapes=scratch
        + [pltpu.SemaphoreType.DMA((copies,)), pltpu.SemaphoreType.DMA((copies,))],
        compiler_params=pltpu.CompilerParams(
            collective_id=0, has_side_effects=True, vmem_limit_bytes=60 * 1024 * 1024
        ),
        name="sum_grads",
    )(*arrays)


def fits(shape, plan):
    for _, dim in plan:
        if shape[dim] % 2:
            return False
        shape = shrink(shape, dim)
    return shape[0] % 16 == 0 and shape[1] % 128 == 0


def per_device(
    dp_size,
    tp_size,
    tokens,
    segment_ids,
    positions,
    norm1_gain,
    qkv_weight,
    out_weight,
    norm2_gain,
    mlp_in_weight,
    mlp_out_weight,
    cotangent,
):
    local_len = segment_ids.shape[0]
    seq_count = local_len // SEQ_LEN
    head_width = out_weight.shape[0]
    head_count = head_width // HEAD_DIM
    own = tokens.shape[0]
    paired = tp_size == 2 and seq_count == 1
    if paired:
        upper = lax.axis_index("tensor") != 0

        def own_first(array):
            return jnp.where(upper, jnp.concatenate([array[own:], array[:own]]), array)

        segment_ids = own_first(segment_ids)
        positions = own_first(positions)

    def gather(rows):
        if paired:
            return jnp.concatenate([rows, swap(rows, "tensor", 2, 1)], axis=0)
        return lax.all_gather(rows, "tensor", axis=0, tiled=True)

    def scatter_sum(product, rows):
        if paired:
            other = swap(product(rows[own:]).astype(jnp.bfloat16), "tensor", 2, 1)
            return product(rows[:own]) + other.astype(jnp.float32)
        return lax.psum_scatter(product(rows), "tensor", scatter_dimension=0, tiled=True)

    bits = [1 << b for b in range(dp_size.bit_length() - 1)]
    power = dp_size == 1 << len(bits) and dp_size >= 4
    wide = (mlp_out_weight.shape[0], tokens.shape[1])
    tall = (qkv_weight.shape[1] * tokens.shape[1] // 2, head_width)
    flat = (head_width // 2, tokens.shape[1])
    orders = (bits, bits[1::-1] + bits[2:], bits[2:3] + bits[:2] + bits[3:])

    def plan_of(order, dims):
        return tuple((bit, dims[min(i, len(dims) - 1)]) for i, bit in enumerate(orders[order]))

    wide_plans = [plan_of(order, (1, 1, 1, 0)) for order in range(3)]
    row_plans = [plan_of(order, (0,)) for order in range(2)]
    kernel_way = (
        power
        and all(fits(wide, plan) for plan in wide_plans)
        and all(fits(tall, plan) and fits(flat, plan) for plan in row_plans)
    )
    early = 2

    def total(array, plan):
        if power:
            return sum_over(array, "dp", dp_size, plan)
        return lax.psum(array, "dp")

    def split_seq(array):
        return array.reshape((seq_count, SEQ_LEN) + array.shape[1:])

    full_cot = gather(cotangent)
    token_f32 = tokens.astype(jnp.float32)
    normed_one, spread_one = norm_rows(token_f32)
    attn_in = (normed_one * norm1_gain).astype(jnp.bfloat16)
    full_one = gather(attn_in)
    projected = [
        jnp.dot(full_one, qkv_weight[:, c], preferred_element_type=jnp.float32) for c in range(3)
    ]
    cos_table, sin_table = rope_tables(positions)
    query = rotate(
        projected[0].reshape(local_len, head_count, HEAD_DIM), cos_table, sin_table
    ).astype(jnp.bfloat16)
    key_rot = rotate(
        projected[1].reshape(local_len, head_count, HEAD_DIM), cos_table, sin_table
    ).astype(jnp.bfloat16)
    value = projected[2].reshape(local_len, head_count, HEAD_DIM).astype(jnp.bfloat16)

    def attend_item(item):
        return attend(item[0], item[1], item[2], item[3])

    attended, log_total = lax.map(
        attend_item,
        (split_seq(query), split_seq(key_rot), split_seq(value), split_seq(segment_ids)),
    )
    attended = attended.reshape(local_len, head_count, HEAD_DIM)
    attn_flat = attended.reshape(local_len, head_width)
    resid_mid = token_f32 + scatter_sum(
        lambda rows: jnp.dot(rows, out_weight, preferred_element_type=jnp.float32), attn_flat
    )
    normed_two, spread_two = norm_rows(resid_mid)
    mlp_in = (normed_two * norm2_gain).astype(jnp.bfloat16)
    full_two = gather(mlp_in)
    gate_pre = jnp.dot(full_two, mlp_in_weight[:, 0], preferred_element_type=jnp.float32)
    up_part = jnp.dot(full_two, mlp_in_weight[:, 1], preferred_element_type=jnp.float32)
    cdf = 0.5 * (1.0 + jax.scipy.special.erf(gate_pre * (1.0 / math.sqrt(2.0))))
    activated = gate_pre * cdf
    hidden = (activated * up_part).astype(jnp.bfloat16)

    grad_w2 = contract_rows(hidden, full_cot).astype(jnp.bfloat16)
    grad_hidden = contract_cols(full_cot, mlp_out_weight)
    slope = cdf + gate_pre * jnp.exp(-0.5 * gate_pre * gate_pre) * INV_ROOT_TWO_PI
    grad_gate = (grad_hidden * up_part * slope).astype(jnp.bfloat16)
    grad_up = (grad_hidden * activated).astype(jnp.bfloat16)
    wide_grads = [
        grad_w2,
        contract_rows(grad_gate, full_two).astype(jnp.bfloat16),
        contract_rows(grad_up, full_two).astype(jnp.bfloat16),
    ]
    if kernel_way:
        pending = [
            halve(grad, "dp", dp_size, *plan[0]) for grad, plan in zip(wide_grads, wide_plans)
        ]
    output = (
        resid_mid
        + scatter_sum(
            lambda rows: jnp.dot(rows, mlp_out_weight, preferred_element_type=jnp.float32), hidden
        )
    ).astype(jnp.bfloat16)
    grad_gu = jnp.concatenate([grad_gate, grad_up], axis=1)

    def back_mlp(rows):
        width = grad_gate.shape[1]
        return contract_cols(rows[:, :width], mlp_in_weight[:, 0]) + contract_cols(
            rows[:, width:], mlp_in_weight[:, 1]
        )

    grad_mlp_in = scatter_sum(back_mlp, grad_gu)
    grad_gain_two = jnp.sum(grad_mlp_in * normed_two, axis=0)
    grad_mid = cotangent.astype(jnp.float32) + norm_back(
        grad_mlp_in * norm2_gain, normed_two, spread_two
    )
    full_mid = gather(grad_mid.astype(jnp.bfloat16))
    grad_wo = contract_rows(attn_flat, full_mid).astype(jnp.bfloat16)
    grad_att = contract_cols(full_mid, out_weight).astype(jnp.bfloat16)
    grad_att = grad_att.reshape(local_len, head_count, HEAD_DIM)

    def back_item(item):
        return attend_back(item[0], item[1], item[2], item[3], item[4], item[5], item[6])

    grad_query, grad_key, grad_value = lax.map(
        back_item,
        (
            split_seq(query),
            split_seq(key_rot),
            split_seq(value),
            split_seq(attended),
            split_seq(grad_att),
            log_total,
            split_seq(segment_ids),
        ),
    )
    grad_query = grad_query.reshape(local_len, head_count, HEAD_DIM)
    grad_key = grad_key.reshape(local_len, head_count, HEAD_DIM)
    grad_proj = jnp.concatenate(
        [
            unrotate(grad_query, cos_table, sin_table).reshape(local_len, head_width),
            unrotate(grad_key, cos_table, sin_table).reshape(local_len, head_width),
            grad_value.reshape(local_len, head_width),
        ],
        axis=1,
    ).astype(jnp.bfloat16)
    if kernel_way:
        pending, grad_proj = lax.optimization_barrier((pending, grad_proj))
        pending = [
            halve(add_halves(*pair), "dp", dp_size, *plan[1])
            for pair, plan in zip(pending, wide_plans)
        ]
    grad_wqkv = jnp.concatenate(
        [
            contract_rows(full_one, grad_proj[:, c * head_width : (c + 1) * head_width])
            for c in range(3)
        ],
        axis=0,
    ).astype(jnp.bfloat16)
    def back_qkv(rows):
        return sum(
            contract_cols(rows[:, c * head_width : (c + 1) * head_width], qkv_weight[:, c])
            for c in range(3)
        )

    grad_attn_in = scatter_sum(back_qkv, grad_proj)
    grad_gain_one = jnp.sum(grad_attn_in * normed_one, axis=0)
    input_grad = (grad_mid + norm_back(grad_attn_in * norm1_gain, normed_one, spread_one)).astype(
        jnp.bfloat16
    )
    row_grads = [
        grad_wo[: flat[0]],
        grad_wo[flat[0] :],
        grad_wqkv[: tall[0]],
        grad_wqkv[tall[0] :],
    ]
    plans = wide_plans + [row_plans[0], row_plans[1]] * 2
    gains = jnp.stack([grad_gain_one, grad_gain_two])
    if kernel_way:
        gains = gains + swap(gains, "tensor", 2, 1) if tp_size == 2 else lax.psum(gains, "tensor")
        gains = gains.reshape(-1, 128)
        used = gains.shape[0]
        gains = jnp.pad(gains, ((0, -used % (8 * dp_size)), (0, 0)))
        parts = [add_halves(*pair) for pair in pending] + row_grads + [gains]
        sums = kernel_sums("dp", parts, plans + [row_plans[0]], [early] * 3 + [0] * 5)
        gains = sums[-1][:used].reshape(2, -1)
    else:
        gains = lax.psum(gains, ("dp", "tensor"))
        sums = [total(grad, plan) for grad, plan in zip(wide_grads + row_grads, plans)]
    grad_w2 = sums[0].astype(jnp.float32)
    grad_w1 = jnp.stack(sums[1:3]).transpose(2, 0, 1).astype(jnp.float32)
    grad_wo = jnp.concatenate(sums[3:5], axis=0).astype(jnp.float32)
    grad_wqkv = jnp.concatenate(sums[5:7], axis=0).reshape(3, -1, head_width)
    grad_wqkv = grad_wqkv.transpose(1, 0, 2).astype(jnp.float32)
    return (output, input_grad, gains[0], grad_wqkv, grad_wo, gains[1], grad_w1, grad_w2)


def solution(mesh):
    body = functools.partial(per_device, mesh.shape["dp"], mesh.shape["tensor"])
    return jax.shard_map(
        body,
        mesh=mesh,
        in_specs=(
            P(("dp", "tensor"), None),
            P("dp"),
            P("dp"),
            P(),
            P(None, None, "tensor"),
            P("tensor", None),
            P(),
            P(None, None, "tensor"),
            P("tensor", None),
            P(("dp", "tensor"), None),
        ),
        out_specs=(
            P(("dp", "tensor"), None),
            P(("dp", "tensor"), None),
            P(),
            P(None, None, "tensor"),
            P("tensor", None),
            P(),
            P(None, None, "tensor"),
            P("tensor", None),
        ),
        check_vma=False,
    )
```
